256 devices in a mesh: rows: 64 (over z, x, core), cols: 4 (over y).
Axes of the slice: x: 4, y: 4, z: 8, core: 2. Of those that a mesh axis runs over, the one named last changes fastest.
Arguments:
- front_rows: bfloat16 [8, 8192, 4096], P(None, 'rows', 'cols'), may hold values from -0.0625 to 0.0625
- heights: int32 [64, 8], P('rows'), may hold values from 1 to 128
- child_rows: bfloat16 [65536, 4096], P('rows', 'cols'), may hold values from -0.0625 to 0.0625
- child_dest: int32 [65536, 1], P('rows'), may hold values from 0 to 63; in each aligned block of 1024 rows (0 to 1023, 1024 to 2047, ...) at most 32 rows name the same one
- child_slot: int32 [65536], P('rows'), may hold values from 0 to 127
- parent_ids: int32 [1024], P('rows'), may hold values from 0 to 7
Outputs:
- r_rows: float32 [8, 128, 4096], P(None, None, ('cols', 'rows'))
The draws below stay inside these ranges and needn't reach their ends.
Inputs may be any that keep to these rules, and one draw needn't show every extreme that they name: `child_dest`: in the rows of one device, at most 32 child rows name one index of rows.
All inputs are finite; a program needn't handle non-finite values.
Results may differ from the reference program's by a relative error of at most 0.002.
Values may be sent and summed in bfloat16 or wider, within the bound.
No kernel may reach another device: no remote copies, remote signals or barrier semaphores. Data moves between devices by JAX's collectives and lax.ppermute only.
A program may use at most 64 MiB of HBM per device.

```python
import math
import jax
import jax.numpy as jnp
import numpy as np
from jax import lax

W = 4096
NB = 128
F = 8
HC = 128
CR = 1024
KB = 64
CAP = 32
KIDS = 1024
N_ROWS = 64


def draw_heights(key, part):
    key_shift, key_spot = jax.random.split(jax.random.fold_in(key, 17), 2)
    halving = jax.random.randint(key_shift, (N_ROWS * F,), 0, 4)
    values = jnp.maximum(1, HC // jnp.power(2, halving))
    spot = jax.random.randint(key_spot, (), 0, N_ROWS * F)
    values = jnp.where(jnp.arange(N_ROWS * F) == spot, HC, values)
    return values.reshape(N_ROWS, F).astype(jnp.int32)


def with_ends(array, stream_key, least, high):
    longest = array.shape.index(max(array.shape))
    spots = []
    for shift in (0, 1):
        where = [jax.random.randint(jax.random.fold_in(stream_key, axis), (), 0, length) for axis, length in enumerate(array.shape)]
        where[longest] = (where[longest] + shift) % array.shape[longest]
        spots.append(tuple(where))
    return array.at[spots[0]].set(least).at[spots[1]].set(high)


def levels(key, extent, cuts, least, high):
    factor_of, own = 1.0, jax.random.fold_in(key, 6)
    for position, blocks in cuts:
        steps = jnp.exp(jax.random.uniform(jax.random.fold_in(own, position), (blocks,), jnp.float32, least / len(cuts), high / len(cuts)))
        factor_of = factor_of * jnp.repeat(steps, extent[position] // blocks).reshape([-1 if axis == position else 1 for axis in range(len(extent))])
    return factor_of


def deal_out(key, own, number, rows, count, top, limit, skew):
    sequence = jax.random.permutation(key, count)
    crowded, common = shares(count, rows * top, limit, skew, True), shares(count, rows * top, limit, skew, False)
    places = jnp.arange(count)

    def named(sizes, offset_by):
        used = int((sizes > 0).sum())
        fixed = max(1, used // 4)
        passed = fixed + (places - fixed + offset_by * (used - fixed)) % max(1, count - fixed)
        return jnp.zeros((count,), jnp.int32).at[sequence[jnp.where(places < fixed, places, passed)]].set(jnp.asarray(sizes, jnp.int32))

    sizes = jnp.where(number % 4 == 0, named(crowded, number // 4), named(common, number - number // 4 - 1))
    mixed = jax.random.permutation(jax.random.fold_in(own, 3), count)
    giver, taker = mixed[0:count // 2 * 2:2], mixed[1:count // 2 * 2:2]
    margin = jnp.minimum(sizes[giver] - 1, limit - sizes[taker]) // 2
    margin = jnp.where((giver == sequence[0]) | (taker == sequence[0]) | (sizes[taker] == 0), 0, jnp.maximum(margin, 0))
    passed = jax.random.randint(jax.random.fold_in(own, 4), (count // 2,), 0, 1 << 20) % (margin + 1)
    sizes = sizes.at[giver].add(-passed).at[taker].add(passed)
    items = jnp.searchsorted(jnp.cumsum(sizes), jnp.arange(rows * top), side="right").astype(jnp.int32)
    listing = items.reshape(top, rows).T
    listing = listing[jax.random.permutation(jax.random.fold_in(own, 1), rows)]
    offset_by = jax.random.randint(jax.random.fold_in(own, 2), (rows, 1), 0, top)
    return jnp.take_along_axis(listing, (jnp.arange(top)[None, :] + offset_by) % top, axis=1)


def shares(number_of, total, reach, skew, full):
    weights = [(1 << 20) // math.isqrt(rank ** skew) + 1 for rank in range(1, number_of + 1)]
    largest = reach if full else min(reach, max(-(-total // number_of), total * weights[0] // sum(weights)))
    least = 1 if total - largest >= number_of - 1 else 0
    counts, spare = [largest] + [least] * (number_of - 1), total - largest - least * (number_of - 1)
    while spare > 0:
        free = [i for i in range(1, number_of) if counts[i] < largest] or [i for i in range(1, number_of) if counts[i] < reach]
        whole, budget = sum([weights[i] for i in free]), spare
        for i in free:
            more = min(reach - counts[i], max(1, budget * weights[i] // whole), spare)
            counts[i] = counts[i] + more
            spare = spare - more
    return np.array(counts)


def gaussian(stream_key, extent, width, limit, shards=(), held_as=jnp.bfloat16):
    result = jax.random.normal(stream_key, extent, jnp.float32) * width
    if len(shards) > 0:
        result = levels(stream_key, extent, shards, -0.22, 0.18) * result
    return jnp.clip(result, min=-limit, max=limit).astype(held_as)


def setup_inputs(seed: int = 0) -> dict:
    splits = jax.random.split(jax.random.key(seed), 7)
    front_rows = gaussian(splits[0], (F, N_ROWS * HC, W), ((N_ROWS * HC) ** -0.5), 0.0625, ((1, 64), (2, 4)))
    heights = draw_heights(jax.random.fold_in(splits[6], 71), 0)
    child_rows = gaussian(splits[2], (N_ROWS * CR, W), ((N_ROWS * HC) ** -0.5), 0.0625, ((0, 64), (1, 4)))
    child_dest_keys = jax.random.split(jax.random.fold_in(splits[3], 1), (N_ROWS * CR) // CR)
    child_dest_turns = jax.random.permutation(jax.random.fold_in(splits[3], 3), (N_ROWS * CR) // CR)
    child_dest = jax.vmap(lambda own, number: deal_out(jax.random.fold_in(splits[3], 2), own, number, CR, N_ROWS, 1, CAP, 2))(child_dest_keys, child_dest_turns).reshape((N_ROWS * CR, 1))
    child_slot = with_ends(jax.random.randint(splits[4], (N_ROWS * CR,), 0, HC), jax.random.fold_in(splits[4], 1), 0, HC - 1).astype(jnp.int32)
    parent_ids = with_ends(jax.random.randint(splits[5], (KIDS,), 0, F), jax.random.fold_in(splits[5], 1), 0, F - 1).astype(jnp.int32)
    return {"front_rows": front_rows, "heights": heights, "child_rows": child_rows, "child_dest": child_dest, "child_slot": child_slot, "parent_ids": parent_ids}


def reference(front_rows, heights, child_rows, child_dest, child_slot, parent_ids):
    own_rows = front_rows.reshape(F, N_ROWS, HC, W)
    live_mask = jnp.arange(HC, dtype=jnp.int32)[None, None, :] < jnp.transpose(heights)[:, :, None]
    child_front = jnp.repeat(parent_ids, KB)
    target = child_dest[:, 0] * HC + child_slot
    child_lead = child_rows[:, :NB].astype(jnp.float32)

    def one_front(front):
        base = jnp.where(live_mask[front][:, :, None], own_rows[front], jnp.zeros((), jnp.bfloat16))
        base = base.reshape(N_ROWS * HC, W)
        belongs = child_front == front
        weight = belongs.astype(jnp.float32)
        added = jnp.zeros((N_ROWS * HC, NB), jnp.float32).at[target].add(child_lead * weight[:, None])
        panel = (base[:, :NB].astype(jnp.float32) + added).astype(jnp.bfloat16)
        picked = jnp.where(belongs[:, None], panel[target], jnp.zeros((), jnp.bfloat16))
        cross = jnp.dot(panel.T.astype(jnp.float32), base.astype(jnp.float32), preferred_element_type=jnp.float32)
        cross = cross + jnp.dot(picked.T.astype(jnp.float32), child_rows.astype(jnp.float32), preferred_element_type=jnp.float32)
        gram = jnp.dot(panel.T.astype(jnp.float32), panel.astype(jnp.float32), preferred_element_type=jnp.float32)
        lower = jnp.linalg.cholesky(gram)
        return jax.scipy.linalg.solve_triangular(lower, cross, lower=True)
    return lax.map(one_front, jnp.arange(F, dtype=jnp.int32))
```

```python
import jax
import jax.numpy as jnp
from jax import lax
from jax.experimental import pallas as pl
from jax.experimental.pallas import tpu as pltpu
from jax.sharding import PartitionSpec as P

NB = 128
CORES = 2
X = 4
BF = jnp.bfloat16
F32 = jnp.float32
I32 = jnp.int32


def dot(a, b, ca, cb, precision=None):
    return lax.dot_general(
        a, b, (((ca,), (cb,)), ((), ())), precision=precision, preferred_element_type=F32
    )


def iota(shape, axis):
    return lax.broadcasted_iota(I32, shape, axis)


def onehot(mask):
    return jnp.where(mask, 1.0, 0.0).astype(BF)


def vmem(n):
    return [pl.BlockSpec(memory_space=pltpu.VMEM)] * n


def call(kernel, outs, in_specs, scratch=(), flops=1 << 20, name=None):
    return pl.pallas_call(
        kernel,
        out_shape=outs,
        in_specs=in_specs,
        out_specs=jax.tree.map(lambda _: pl.BlockSpec(memory_space=pltpu.VMEM), outs),
        scratch_shapes=scratch,
        cost_estimate=pl.CostEstimate(flops=flops, bytes_accessed=1 << 20, transcendentals=0),
        name=name,
    )


SMEM = pl.BlockSpec(memory_space=pltpu.SMEM)


def lead_kernel(child_ref, front_ref, heights_ref, out_ref):
    eye = onehot(iota((NB, NB), 0) == iota((NB, NB), 1))
    quarter = out_ref.shape[1] // 2
    child = dot(eye, child_ref[...], 1, 1).astype(BF)
    for c in range(out_ref.shape[0]):
        out_ref[c, :quarter] = child[c * quarter : (c + 1) * quarter]
    for f in range(front_ref.shape[0]):
        own = dot(eye, front_ref[f], 1, 1)
        own = jnp.where(iota(own.shape, 1) < heights_ref[0, f], own, 0.0).astype(BF)
        for c in range(out_ref.shape[0]):
            out_ref[c, quarter:, f * NB : (f + 1) * NB] = own[c * quarter : (c + 1) * quarter]


def index_kernel(peers, capacity, groups, dest_ref, key_ref):
    count = dest_ref.shape[1]
    dest = dest_ref[...]
    hits = onehot(iota((peers, count), 0) == dest)
    upper = onehot(iota((NB, NB), 0) < iota((NB, NB), 1))
    offset = jnp.zeros((peers, 1), F32)
    per = capacity // groups
    for b in range(count // NB):
        block = hits[:, b * NB : (b + 1) * NB]
        before = dot(block, upper, 1, 0) + offset
        block = block.astype(F32)
        position = jnp.sum(before * block, axis=0, keepdims=True).astype(I32)
        offset = offset + jnp.sum(block, axis=1, keepdims=True)
        where_to = dest[:, b * NB : (b + 1) * NB]
        key_ref[:, b * NB : (b + 1) * NB] = (
            (position // per) * (peers * per) + where_to * per + position % per
        )


def quarter_of(col, parts, low, high):
    base = parts[0][0, low:high].astype(F32)
    total = jnp.where(col == 0, base, jnp.zeros_like(base))
    for part in parts[1:]:
        total = total + part[low:high].astype(F32)
    return total


def placed(block, q, groups):
    rows = block.shape[0]
    pieces = []
    if q:
        pieces.append(jnp.zeros((q * rows, block.shape[1]), block.dtype))
    pieces.append(block)
    if q < groups - 1:
        pieces.append(jnp.zeros(((groups - 1 - q) * rows, block.shape[1]), block.dtype))
    return jnp.concatenate(pieces, axis=0)


def pack_kernel(col_ref, parent_ref, key_ref, slot_ref, p0, p1, p2, p3, out_ref):
    groups = 4
    quarter = NB // groups
    count = key_ref.shape[1]
    peers = out_ref.shape[0]
    per = out_ref.shape[1] // 2
    lead = quarter_of(col_ref[0], (p0, p1, p2, p3), 0, quarter).astype(BF)
    lane = iota((1, count), 1)
    kb = count // parent_ref.shape[0]
    front = jnp.zeros((1, count), I32)
    for b in range(parent_ref.shape[0]):
        front = jnp.where(lane // kb == b, parent_ref[b], front)
    slot = slot_ref[...].astype(F32)
    front = front.astype(F32)
    key = key_ref[...]
    total = jnp.zeros((peers * per, 2 * NB), F32)
    rows = iota((NB, count), 0)
    for q in range(groups):
        meta = jnp.where(rows == q, slot, jnp.where(rows == groups + q, front, 0.0)).astype(BF)
        source = jnp.concatenate([placed(lead, q, groups), meta], axis=0)
        hit = onehot(iota((peers * per, count), 0) + q * peers * per == key)
        total = total + dot(hit, source, 1, 1)
    data = total[:, :NB].reshape(peers, per, NB)
    meta = total[:, NB:].reshape(peers, per, NB)
    out_ref[...] = jnp.concatenate([data, meta], axis=1).astype(BF)


def panel_kernel(col_ref, got_ref, p0, p1, p2, p3, panel_ref, back_ref, hit_ref):
    groups = 4
    quarter = NB // groups
    peers, twice, _ = got_ref.shape
    per = twice // 2
    targets = panel_ref.shape[1]
    got = got_ref[...].astype(F32)
    data = got[:, :per].reshape(peers * per, NB)
    meta = got[:, per:].reshape(peers * per, NB)
    target = (meta + NB * pltpu.roll(meta, NB - groups, 1)).astype(I32)
    turned = data.T.astype(BF)
    total = quarter_of(col_ref[0], (p0, p1, p2, p3), quarter, 2 * quarter)
    for q in range(groups):
        hit_ref[q] = onehot(iota((peers * per, targets), 1) == target[:, q : q + 1])
        total = total + dot(turned[q * quarter : (q + 1) * quarter], hit_ref[q], 1, 0)
    panel = total.astype(BF)
    panel_ref[...] = panel
    back = jnp.zeros((peers * per, NB), F32)
    for q in range(groups):
        back = back + dot(hit_ref[q], placed(panel, q, groups), 1, 1)
    back_ref[...] = back.reshape(peers, per, NB).astype(BF)


def pick_kernel(key_ref, got_ref, out_ref):
    groups = 4
    quarter = NB // groups
    peers, per, _ = got_ref.shape
    count = key_ref.shape[1]
    turned = got_ref[...].astype(F32).reshape(peers * per, NB).T.astype(BF)
    key = key_ref[...]
    total = jnp.zeros((quarter, count), F32)
    for q in range(groups):
        hit = onehot(iota((peers * per, count), 0) + q * peers * per == key)
        total = total + dot(turned[q * quarter : (q + 1) * quarter], hit, 1, 0)
    out_ref[...] = total.astype(BF)


def turn_kernel(core_ref, child_ref, front_ref, out_ref):
    halves, xs, zs, run, _ = out_ref.shape
    row, column = iota((NB, NB), 0), iota((NB, NB), 1)
    half = row // (xs * run)
    core = jnp.where(half == 0, 1 - core_ref[0], core_ref[0])
    pick = onehot(column == ((row // run) % xs) * (CORES * run) + core * run + row % run)
    count = child_ref.shape[0]
    for z in range(zs):
        turned = dot(pick, child_ref[:, z * NB : (z + 1) * NB], 1, 1).astype(BF)
        own = [
            dot(pick, front_ref[f, :, z * NB : (z + 1) * NB], 1, 1).astype(BF)
            for f in range(front_ref.shape[0])
        ]
        turned = jnp.concatenate(own + [turned], axis=1)
        for h in range(halves):
            for x in range(xs):
                low = (h * xs + x) * run
                out_ref[h, x, z] = turned[low : low + run]


def ring_into(col, parts, whole):
    n = len(parts)
    for d in range(n):
        whole[lax.rem(col - d + n, n)] = parts[d][...]


def cross_kernel(
    half, col_ref, parent_ref, heights_ref, rows_ref,
    a0, a1, a2, a3, b0, b1, b2, b3, out_ref, panel_ref, picked_ref
):
    fronts = heights_ref.shape[1]
    col = col_ref[0]
    ring_into(col, (a0, a1, a2, a3), panel_ref)
    ring_into(col, (b0, b1, b2, b3), picked_ref)
    count = picked_ref.shape[2]
    own = fronts * NB
    panel = panel_ref[...].reshape(NB, own)
    picked = picked_ref[...].reshape(NB, count)
    kb = count // parent_ref.shape[0]
    lane = iota((1, count), 1) // kb
    front = jnp.zeros((1, count), I32)
    for b in range(parent_ref.shape[0]):
        front = jnp.where(lane == b, parent_ref[b], front)
    height = iota((NB, NB), 1)
    rows = rows_ref[...].reshape(-1, own + count)
    zero = jnp.zeros((NB, NB), BF)
    for f in range(0, fronts, 2):
        owns, kids = [], []
        for g in (f, f + 1):
            block = panel[:, g * NB : (g + 1) * NB]
            block = jnp.where(height < heights_ref[0, g], block, zero)
            owns.append(jnp.concatenate([block, zero] if g == f else [zero, block], axis=1))
            kids.append(jnp.where(front == g, picked, jnp.zeros_like(picked)))
        weights = jnp.concatenate(
            [jnp.concatenate(owns, axis=0), jnp.concatenate(kids, axis=0)], axis=1
        )
        left = jnp.concatenate([rows[:, f * NB : (f + 2) * NB], rows[:, own:]], axis=1)
        out_ref[:, f * NB : (f + 2) * NB] = dot(left, weights, 1, 1)


def gram_kernel(col_ref, a0, a1, a2, a3, out_ref, panel_ref):
    ring_into(col_ref[0], (a0, a1, a2, a3), panel_ref)
    panel = panel_ref[...].reshape(NB, panel_ref.shape[2])
    for f in range(out_ref.shape[0] // NB):
        block = panel[:, f * NB : (f + 1) * NB]
        out_ref[f * NB : (f + 1) * NB] = dot(block, block, 1, 1)


def factor_kernel(gram_ref, out_ref, a_ref):
    n = gram_ref.shape[0]
    row, column = iota((NB, NB), 0), iota((NB, NB), 1)
    for f in range(n):
        a_ref[f] = gram_ref[f]
        out_ref[f] = jnp.where(row == column, 1.0, 0.0)

    def block(t, carry):
        for j in range(8):
            for f in range(n):
                a = a_ref[f]
                pivot_rows = a_ref[f, pl.ds(t * 8, 8), :]
                pivot_row = pivot_rows[j : j + 1]
                inverse_rows = out_ref[f, pl.ds(t * 8, 8), :]
                inverse_row = inverse_rows[j : j + 1]
                factor = a[:, j : j + 1] * (1.0 / pivot_row[:, j : j + 1])
                factor = jnp.where(row[:, :1] > t * 8 + j, factor, 0.0)
                a_ref[f] = a - factor * pivot_row
                out_ref[f] = out_ref[f] - factor * inverse_row
        for f in range(n):
            rows = a_ref[f, pl.ds(t * 8, 8), :]
            eye = iota((8, NB), 0) == iota((8, NB), 1)
            d = jnp.sum(jnp.where(eye, rows, 0.0), axis=1, keepdims=True)
            out_ref[f, pl.ds(t * 8, 8), :] = out_ref[f, pl.ds(t * 8, 8), :] * lax.rsqrt(d)
            a_ref[f] = pltpu.roll(a_ref[f], NB - 8, 1)
        return carry

    lax.fori_loop(0, NB // 8, block, 0)


def solve_kernel(col_ref, cross_ref, i0, i1, i2, i3, out_ref, inverse_ref):
    ring_into(col_ref[0], (i0, i1, i2, i3), inverse_ref)
    total = jnp.sum(cross_ref[...], axis=0)
    n = inverse_ref.shape[1]
    for f in range(out_ref.shape[0]):
        out_ref[f] = dot(
            total[:, f * NB : (f + 1) * NB], inverse_ref[f // n, f % n], 1, 1,
            precision=lax.Precision.HIGHEST,
        )


def on_device(front_rows, heights, child_rows, child_dest, child_slot, parent_ids):
    fronts, height_cap, width = front_rows.shape
    peers = lax.axis_size("rows")
    cols = lax.axis_size("cols")
    count = child_rows.shape[0]
    zs = peers // (X * CORES)
    capacity = max(2, 2 * count // peers)
    quarter = NB // cols
    per = capacity * quarter // NB
    run = width // peers
    targets = fronts * height_cap
    sds = jax.ShapeDtypeStruct

    col = lax.axis_index("cols")[None]
    core = (lax.axis_index("rows") % CORES)[None]

    def spread(value, shifts=range(1, 4)):
        return [value] + [
            lax.ppermute(value, "cols", [(i, (i + d) % cols) for i in range(cols)])
            for d in shifts
        ]

    dest = child_dest.reshape(1, count)
    slot = child_slot.reshape(1, count)

    lead = pl.pallas_call(
        lead_kernel,
        grid=(1,),
        out_shape=sds((cols, 2 * quarter, count), BF),
        in_specs=[
            pl.BlockSpec((count, NB), lambda i: (0, 0)),
            pl.BlockSpec((fronts, height_cap, NB), lambda i: (0, 0, 0)),
            SMEM,
        ],
        out_specs=pl.BlockSpec((cols, 2 * quarter, count), lambda i: (0, 0, 0)),
        name="lead",
    )(child_rows, front_rows, heights)
    parts = [lead] + [lax.ppermute(lead[d], "cols", [(0, d)]) for d in range(1, cols)]

    key = call(
        lambda *r: index_kernel(peers, capacity, cols, *r), sds((1, count), I32), vmem(1),
        name="index",
    )(dest)
    send = call(
        pack_kernel, sds((peers, 2 * per, NB), BF), [SMEM, SMEM] + vmem(6), name="pack"
    )(col, parent_ids, key, slot, *parts)
    got = lax.all_to_all(send, "rows", 0, 0, tiled=True)

    rows = call(
        turn_kernel, sds((CORES, X, zs, run, targets + count), BF), [SMEM] + vmem(2),
        flops=1 << 29, name="turn",
    )(core, child_rows, front_rows)

    panel, back = call(
        panel_kernel,
        (sds((quarter, targets), BF), sds((peers, per, NB), BF)),
        [SMEM] + vmem(5),
        [pltpu.VMEM((cols, peers * per, targets), BF)],
        name="panel",
    )(col, got, *parts)
    returned = lax.all_to_all(back, "rows", 0, 0, tiled=True)
    panels = spread(panel)

    whole = [pltpu.VMEM((cols, quarter, targets), BF)]
    gram = call(gram_kernel, sds((fronts * NB, NB), F32), [SMEM] + vmem(4), whole, name="gram")(
        col, *panels
    )
    share = fronts // cols * NB
    mine = lax.dynamic_slice_in_dim(gram, col[0] * share, share, 0)
    sums = lax.all_to_all(mine.reshape(peers, share // peers, NB), "rows", 0, 0, tiled=True)
    sums = jnp.sum(sums, axis=0)
    sums = lax.all_to_all(
        jnp.broadcast_to(sums[None], (peers, share // peers, NB)), "rows", 0, 0, tiled=True
    )
    inverse = call(
        factor_kernel, sds((fronts // cols, NB, NB), F32), vmem(1),
        [pltpu.VMEM((fronts // cols, NB, NB), F32)], flops=1 << 28, name="factor",
    )(sums.reshape(fronts // cols, NB, NB))
    inverses = spread(inverse)

    picked = call(pick_kernel, sds((quarter, count), BF), vmem(2), name="pick")(key, returned)
    pickeds = spread(picked)

    halves = []
    for h in range(CORES):
        halves.append(
            call(
                lambda *r, h=h: cross_kernel(h, *r),
                sds((X * zs * run, targets), F32),
                [SMEM, SMEM, SMEM] + vmem(9),
                [
                    pltpu.VMEM((cols, quarter, targets), BF),
                    pltpu.VMEM((cols, quarter, count), BF),
                ],
                flops=1 << 31,
                name="cross%d" % h,
            )(col, parent_ids, heights, rows[h], *panels, *pickeds)
        )
    other = lax.ppermute(halves[0], "rows", [(i, i ^ 1) for i in range(peers)])
    chip = (halves[1] + other).reshape(X, zs * run, targets)

    def at(z, x, c):
        return (z * X + x) * CORES + c

    over_x = [[at(z, x, c) for x in range(X)] for z in range(zs) for c in range(CORES)]
    over_z = [[at(z, x, c) for z in range(zs)] for x in range(X) for c in range(CORES)]
    chip = lax.all_to_all(chip, "rows", 0, 0, axis_index_groups=over_x, tiled=True)
    chip = jnp.sum(chip, axis=0).reshape(zs, run, targets)
    chip = lax.all_to_all(chip, "rows", 0, 0, axis_index_groups=over_z, tiled=True)

    out = call(
        solve_kernel, sds((fronts, run, NB), F32), [SMEM] + vmem(5),
        [pltpu.VMEM((cols, fronts // cols, NB, NB), F32)], name="solve",
    )(col, chip, *inverses)
    return jnp.transpose(out, (0, 2, 1))


def solution(mesh):
    placed_as = (
        P(None, "rows", "cols"),
        P("rows", None),
        P("rows", "cols"),
        P("rows", None),
        P("rows"),
        P("rows"),
    )
    return jax.shard_map(
        on_device,
        mesh=mesh,
        in_specs=placed_as,
        out_specs=P(None, None, ("cols", "rows")),
        check_vma=False,
    )
```

```python
import jax
import jax.numpy as jnp
from jax import lax
from jax.experimental import pallas as pl
from jax.experimental.pallas import tpu as pltpu
from jax.sharding import PartitionSpec as P

NB = 128
CORES = 2
LIMIT = 30 << 20
X = 4
BF = jnp.bfloat16
F32 = jnp.float32
I32 = jnp.int32


def dot(a, b, ca, cb, precision=None):
    return lax.dot_general(
        a, b, (((ca,), (cb,)), ((), ())), precision=precision, preferred_element_type=F32
    )


def iota(shape, axis):
    return lax.broadcasted_iota(I32, shape, axis)


def onehot(mask):
    return jnp.where(mask, 1.0, 0.0).astype(BF)


def vmem(n):
    return [pl.BlockSpec(memory_space=pltpu.VMEM)] * n


def call(kernel, outs, in_specs, scratch=(), flops=1 << 20, name=None):
    return pl.pallas_call(
        kernel,
        out_shape=outs,
        in_specs=in_specs,
        out_specs=jax.tree.map(lambda _: pl.BlockSpec(memory_space=pltpu.VMEM), outs),
        scratch_shapes=scratch,
        cost_estimate=pl.CostEstimate(flops=flops, bytes_accessed=1 << 20, transcendentals=0),
        name=name,
        compiler_params=pltpu.CompilerParams(vmem_limit_bytes=LIMIT),
    )


SMEM = pl.BlockSpec(memory_space=pltpu.SMEM)


def lead_kernel(child_ref, front_ref, heights_ref, *out_refs):
    eye = onehot(iota((NB, NB), 0) == iota((NB, NB), 1))
    quarter = out_refs[0].shape[0] // 2
    child = dot(eye, child_ref[...], 1, 1).astype(BF)
    for c, out_ref in enumerate(out_refs):
        out_ref[:quarter] = child[c * quarter : (c + 1) * quarter]
    for f in range(front_ref.shape[0]):
        own = dot(eye, front_ref[f], 1, 1)
        own = jnp.where(iota(own.shape, 1) < heights_ref[0, f], own, 0.0).astype(BF)
        for c, out_ref in enumerate(out_refs):
            out_ref[quarter:, f * NB : (f + 1) * NB] = own[c * quarter : (c + 1) * quarter]


def index_kernel(peers, capacity, groups, dest_ref, key_ref):
    count = dest_ref.shape[1]
    dest = dest_ref[...]
    hits = onehot(iota((peers, count), 0) == dest)
    upper = onehot(iota((NB, NB), 0) < iota((NB, NB), 1))
    offset = jnp.zeros((peers, 1), F32)
    per = capacity // groups
    for b in range(count // NB):
        block = hits[:, b * NB : (b + 1) * NB]
        before = dot(block, upper, 1, 0) + offset
        block = block.astype(F32)
        position = jnp.sum(before * block, axis=0, keepdims=True).astype(I32)
        offset = offset + jnp.sum(block, axis=1, keepdims=True)
        where_to = dest[:, b * NB : (b + 1) * NB]
        key_ref[:, b * NB : (b + 1) * NB] = (
            (position // per) * (peers * per) + where_to * per + position % per
        )


def quarter_of(col, parts, low, high):
    base = parts[0][low:high].astype(F32)
    total = jnp.where(col == 0, base, jnp.zeros_like(base))
    for part in parts[1:]:
        total = total + part[low:high].astype(F32)
    return total


def placed(block, q, groups):
    rows = block.shape[0]
    pieces = []
    if q:
        pieces.append(jnp.zeros((q * rows, block.shape[1]), block.dtype))
    pieces.append(block)
    if q < groups - 1:
        pieces.append(jnp.zeros(((groups - 1 - q) * rows, block.shape[1]), block.dtype))
    return jnp.concatenate(pieces, axis=0)


def pack_kernel(col_ref, parent_ref, key_ref, slot_ref, p0, p1, p2, p3, out_ref):
    groups = 4
    quarter = NB // groups
    count = key_ref.shape[1]
    peers = out_ref.shape[0]
    per = out_ref.shape[1] // 2
    lead = quarter_of(col_ref[0], (p0, p1, p2, p3), 0, quarter).astype(BF)
    lane = iota((1, count), 1)
    kb = count // parent_ref.shape[0]
    front = jnp.zeros((1, count), I32)
    for b in range(parent_ref.shape[0]):
        front = jnp.where(lane // kb == b, parent_ref[b], front)
    slot = slot_ref[...].astype(F32)
    front = front.astype(F32)
    key = key_ref[...]
    total = jnp.zeros((peers * per, 2 * NB), F32)
    rows = iota((NB, count), 0)
    for q in range(groups):
        meta = jnp.where(rows == q, slot, jnp.where(rows == groups + q, front, 0.0)).astype(BF)
        source = jnp.concatenate([placed(lead, q, groups), meta], axis=0)
        hit = onehot(iota((peers * per, count), 0) + q * peers * per == key)
        total = total + dot(hit, source, 1, 1)
    data = total[:, :NB].reshape(peers, per, NB)
    meta = total[:, NB:].reshape(peers, per, NB)
    out_ref[...] = jnp.concatenate([data, meta], axis=1).astype(BF)


def panel_kernel(col_ref, got_ref, p0, p1, p2, p3, panel_ref, back_ref, hit_ref):
    groups = 4
    quarter = NB // groups
    peers, twice, _ = got_ref.shape
    per = twice // 2
    targets = panel_ref.shape[1]
    got = got_ref[...].astype(F32)
    data = got[:, :per].reshape(peers * per, NB)
    meta = got[:, per:].reshape(peers * per, NB)
    target = (meta + NB * pltpu.roll(meta, NB - groups, 1)).astype(I32)
    turned = data.T.astype(BF)
    total = quarter_of(col_ref[0], (p0, p1, p2, p3), quarter, 2 * quarter)
    for q in range(groups):
        hit_ref[q] = onehot(iota((peers * per, targets), 1) == target[:, q : q + 1])
        total = total + dot(turned[q * quarter : (q + 1) * quarter], hit_ref[q], 1, 0)
    panel = total.astype(BF)
    panel_ref[...] = panel
    back = jnp.zeros((peers * per, NB), F32)
    for q in range(groups):
        back = back + dot(hit_ref[q], placed(panel, q, groups), 1, 1)
    back_ref[...] = back.reshape(peers, per, NB).astype(BF)


def pick_kernel(key_ref, got_ref, out_ref):
    groups = 4
    quarter = NB // groups
    peers, per, _ = got_ref.shape
    count = key_ref.shape[1]
    turned = got_ref[...].astype(F32).reshape(peers * per, NB).T.astype(BF)
    key = key_ref[...]
    total = jnp.zeros((quarter, count), F32)
    for q in range(groups):
        hit = onehot(iota((peers * per, count), 0) + q * peers * per == key)
        total = total + dot(turned[q * quarter : (q + 1) * quarter], hit, 1, 0)
    out_ref[...] = total.astype(BF)


def turn_kernel(core_ref, child_ref, front_ref, *out_refs):
    xs, zs, run, _ = out_refs[0].shape
    row, column = iota((NB, NB), 0), iota((NB, NB), 1)
    half = row // (xs * run)
    core = jnp.where(half == 0, 1 - core_ref[0], core_ref[0])
    pick = onehot(column == ((row // run) % xs) * (CORES * run) + core * run + row % run)
    count = child_ref.shape[0]
    for z in range(zs):
        turned = dot(pick, child_ref[:, z * NB : (z + 1) * NB], 1, 1).astype(BF)
        own = [
            dot(pick, front_ref[f, :, z * NB : (z + 1) * NB], 1, 1).astype(BF)
            for f in range(front_ref.shape[0])
        ]
        turned = jnp.concatenate(own + [turned], axis=1)
        for h, out_ref in enumerate(out_refs):
            for x in range(xs):
                low = (h * xs + x) * run
                out_ref[x, z] = turned[low : low + run]


def ring_into(col, parts, whole):
    n = len(parts)
    for d in range(n):
        whole[lax.rem(col - d + n, n)] = parts[d][...]


def cross_kernel(
    half, col_ref, parent_ref, heights_ref, rows_ref,
    a0, a1, a2, a3, b0, b1, b2, b3, out_ref, panel_ref, picked_ref
):
    fronts = heights_ref.shape[1]
    col = col_ref[0]
    ring_into(col, (a0, a1, a2, a3), panel_ref)
    ring_into(col, (b0, b1, b2, b3), picked_ref)
    count = picked_ref.shape[2]
    own = fronts * NB
    panel = panel_ref[...].reshape(NB, own)
    picked = picked_ref[...].reshape(NB, count)
    kb = count // parent_ref.shape[0]
    lane = iota((1, count), 1) // kb
    front = jnp.zeros((1, count), I32)
    for b in range(parent_ref.shape[0]):
        front = jnp.where(lane == b, parent_ref[b], front)
    height = iota((NB, NB), 1)
    rows = rows_ref[...].reshape(-1, own + count)
    zero = jnp.zeros((NB, NB), BF)
    for f in range(0, fronts, 2):
        owns, kids = [], []
        for g in (f, f + 1):
            block = panel[:, g * NB : (g + 1) * NB]
            block = jnp.where(height < heights_ref[0, g], block, zero)
            owns.append(jnp.concatenate([block, zero] if g == f else [zero, block], axis=1))
            kids.append(jnp.where(front == g, picked, jnp.zeros_like(picked)))
        weights = jnp.concatenate(
            [jnp.concatenate(owns, axis=0), jnp.concatenate(kids, axis=0)], axis=1
        )
        left = jnp.concatenate([rows[:, f * NB : (f + 2) * NB], rows[:, own:]], axis=1)
        out_ref[:, f * NB : (f + 2) * NB] = dot(left, weights, 1, 1)


def gram_kernel(col_ref, a0, a1, a2, a3, out_ref, panel_ref):
    ring_into(col_ref[0], (a0, a1, a2, a3), panel_ref)
    share = out_ref.shape[0]
    for f in range(share // NB):
        low = pl.multiple_of(col_ref[0] * share + f * NB, NB)
        block = panel_ref[:, :, pl.ds(low, NB)].reshape(NB, NB)
        out_ref[f * NB : (f + 1) * NB] = dot(block, block, 1, 1)


def factor_kernel(gram_ref, out_ref, a_ref):
    n = gram_ref.shape[0]
    step = 8
    sub, lane = iota((step, NB), 0), iota((step, NB), 1)
    for f in range(n):
        a_ref[f] = gram_ref[f]
        out_ref[f] = jnp.where(iota((NB, NB), 0) == iota((NB, NB), 1), 1.0, 0.0)
    for t in range(NB // step):
        low, high = t * step, (t + 1) * step
        for f in range(n):
            top, inverse = a_ref[f, low:high, :], out_ref[f, low:high, :]
            diagonal = jnp.zeros((step, 1), F32)
            for j in range(step):
                column = top[:, low + j : low + j + 1]
                pivot = column[j : j + 1]
                factor = jnp.where(sub[:, :1] > j, column / pivot, 0.0)
                diagonal = jnp.where(sub[:, :1] == j, pivot, diagonal)
                top = top - factor * top[j : j + 1]
                inverse = inverse - factor * inverse[j : j + 1]
            scale = lax.rsqrt(diagonal)
            inverse = inverse * scale
            out_ref[f, low:high, :] = inverse
            if high < NB:
                top = jnp.where(lane >= high, top * scale, 0.0)
                change = dot(
                    top,
                    jnp.concatenate([top, inverse], axis=1), 0, 0,
                    precision=lax.Precision.HIGHEST,
                )
                a_ref[f, high:, :] = a_ref[f, high:, :] - change[high:, :NB]
                out_ref[f, high:, :] = out_ref[f, high:, :] - change[high:, NB:]


def solve_kernel(col_ref, cross_ref, i0, i1, i2, i3, out_ref, inverse_ref):
    ring_into(col_ref[0], (i0, i1, i2, i3), inverse_ref)
    total = jnp.sum(cross_ref[...], axis=0)
    n = inverse_ref.shape[1]
    for f in range(out_ref.shape[0]):
        out_ref[f] = dot(
            total[:, f * NB : (f + 1) * NB], inverse_ref[f // n, f % n], 1, 1,
            precision=lax.Precision.HIGHEST,
        )


def on_device(front_rows, heights, child_rows, child_dest, child_slot, parent_ids):
    fronts, height_cap, width = front_rows.shape
    peers = lax.axis_size("rows")
    cols = lax.axis_size("cols")
    count = child_rows.shape[0]
    zs = peers // (X * CORES)
    capacity = max(2, 2 * count // peers)
    quarter = NB // cols
    per = capacity * quarter // NB
    run = width // peers
    targets = fronts * height_cap
    sds = jax.ShapeDtypeStruct

    col = lax.axis_index("cols")[None]
    core = (lax.axis_index("rows") % CORES)[None]

    def spread(value, shifts=range(1, 4)):
        return [value] + [
            lax.ppermute(value, "cols", [(i, (i + d) % cols) for i in range(cols)])
            for d in shifts
        ]

    dest = child_dest.reshape(1, count)
    slot = child_slot.reshape(1, count)

    lead = pl.pallas_call(
        lead_kernel,
        grid=(1,),
        out_shape=[sds((2 * quarter, count), BF)] * cols,
        in_specs=[
            pl.BlockSpec((count, NB), lambda i: (0, 0)),
            pl.BlockSpec((fronts, height_cap, NB), lambda i: (0, 0, 0)),
            SMEM,
        ],
        out_specs=[pl.BlockSpec((2 * quarter, count), lambda i: (0, 0))] * cols,
        name="lead",
    )(child_rows, front_rows, heights)
    parts = [lead[0]] + [lax.ppermute(lead[d], "cols", [(0, d)]) for d in range(1, cols)]

    key = call(
        lambda *r: index_kernel(peers, capacity, cols, *r), sds((1, count), I32), vmem(1),
        name="index",
    )(dest)
    send = call(
        pack_kernel, sds((peers, 2 * per, NB), BF), [SMEM, SMEM] + vmem(6), name="pack"
    )(col, parent_ids, key, slot, *parts)

    rows = call(
        turn_kernel, [sds((X, zs, run, targets + count), BF)] * CORES, [SMEM] + vmem(2),
        flops=1 << 29, name="turn",
    )(core, child_rows, front_rows)

    got = lax.all_to_all(send, "rows", 0, 0, tiled=True)
    got, rows = lax.optimization_barrier((got, rows))
    panel, back = call(
        panel_kernel,
        (sds((quarter, targets), BF), sds((peers, per, NB), BF)),
        [SMEM] + vmem(5),
        [pltpu.VMEM((cols, peers * per, targets), BF)],
        name="panel",
    )(col, got, *parts)
    returned = lax.all_to_all(back, "rows", 0, 0, tiled=True)
    panels = spread(panel)

    whole = [pltpu.VMEM((cols, quarter, targets), BF)]
    share = fronts // cols * NB
    gram = call(gram_kernel, sds((share, NB), F32), [SMEM] + vmem(4), whole, name="gram")(
        col, *panels
    )
    returned, gram = lax.optimization_barrier((returned, gram))
    sums = lax.all_to_all(gram.reshape(peers, share // peers, NB), "rows", 0, 0, tiled=True)
    sums = jnp.sum(sums, axis=0)

    picked = call(pick_kernel, sds((quarter, count), BF), vmem(2), name="pick")(key, returned)
    pickeds = spread(picked)
    pickeds, sums = lax.optimization_barrier((pickeds, sums))

    sums = lax.all_to_all(
        jnp.broadcast_to(sums[None], (peers, share // peers, NB)), "rows", 0, 0, tiled=True
    )
    inverse = call(
        factor_kernel, sds((fronts // cols, NB, NB), F32), vmem(1),
        [pltpu.VMEM((fronts // cols, NB, NB), F32)], flops=1 << 28, name="factor",
    )(sums.reshape(fronts // cols, NB, NB))

    halves = []
    for h in range(CORES):
        halves.append(
            call(
                lambda *r, h=h: cross_kernel(h, *r),
                sds((X * zs * run, targets), F32),
                [SMEM, SMEM, SMEM] + vmem(9),
                [
                    pltpu.VMEM((cols, quarter, targets), BF),
                    pltpu.VMEM((cols, quarter, count), BF),
                ],
                flops=1 << 31,
                name="cross%d" % h,
            )(col, parent_ids, heights, rows[h], *panels, *pickeds)
        )
    other = lax.ppermute(halves[0], "rows", [(i, i ^ 1) for i in range(peers)])
    chip = (halves[1] + other).reshape(X, zs * run, targets)

    def at(z, x, c):
        return (z * X + x) * CORES + c

    over_x = [[at(z, x, c) for x in range(X)] for z in range(zs) for c in range(CORES)]
    over_z = [[at(z, x, c) for z in range(zs)] for x in range(X) for c in range(CORES)]
    chip = lax.all_to_all(chip, "rows", 0, 0, axis_index_groups=over_x, tiled=True)
    chip, inverse = lax.optimization_barrier((chip, inverse))
    inverses = spread(inverse)
    chip = jnp.sum(chip, axis=0).reshape(zs, run, targets)
    chip = lax.all_to_all(chip, "rows", 0, 0, axis_index_groups=over_z, tiled=True)

    out = call(
        solve_kernel, sds((fronts, run, NB), F32), [SMEM] + vmem(5),
        [pltpu.VMEM((cols, fronts // cols, NB, NB), F32)], name="solve",
    )(col, chip, *inverses)
    return jnp.transpose(out, (0, 2, 1))


def solution(mesh):
    placed_as = (
        P(None, "rows", "cols"),
        P("rows", None),
        P("rows", "cols"),
        P("rows", None),
        P("rows"),
        P("rows"),
    )
    return jax.shard_map(
        on_device,
        mesh=mesh,
        in_specs=placed_as,
        out_specs=P(None, None, ("cols", "rows")),
        check_vma=False,
    )
```
